32 devices in a mesh: grp: 2 (over y), ctx: 4 (over z), tp: 2 (over x), sub: 2 (over core).
Axes of the slice: x: 2, y: 2, z: 4, core: 2. Of those that a mesh axis runs over, the one named last changes fastest.
Arguments:
- context: bfloat16 [3072, 2048], P(('grp', 'ctx'), ('tp', 'sub')), parts along dimension 0, may hold values from -24 to 24
- context_pos: int32 [3072], P(('grp', 'ctx')), parts along dimension 0, may hold values from 0 to 1535, each once
- latent_in: bfloat16 [64, 2048], P(('grp', 'ctx')), parts along dimension 0, may hold values from -24 to 24
- latent_start: int32 [2], P('grp'), parts along dimension 0, may hold values from 768 to 1504
- ctx_gain: float32 [2048], replicated, may hold values from 0.25 to 1.75
- lat_gain: float32 [2048], replicated, may hold values from 0.25 to 1.75
- mid_gain: float32 [2048], replicated, may hold values from 0.25 to 1.75
- cross_q: bfloat16 [2048, 2048], P('ctx', ('tp', 'sub')), may hold values from -2 to 2
- cross_k: bfloat16 [2048, 2048], P('ctx', ('tp', 'sub')), may hold values from -2 to 2
- cross_v: bfloat16 [2048, 2048], P('ctx', ('tp', 'sub')), may hold values from -0.125 to 0.125
- cross_out: bfloat16 [2048, 2048], P('ctx', ('tp', 'sub')), may hold values from -0.125 to 0.125
- self_qkv: bfloat16 [2048, 3, 2048], P('ctx', None, ('tp', 'sub')), may hold values from -2 to 2
- self_out: bfloat16 [2048, 2048], P('ctx', ('tp', 'sub')), may hold values from -0.125 to 0.125
Outputs:
- latent_out: bfloat16 [64, 2048], P(('grp', 'ctx'), ('tp', 'sub')), parts along dimension 0
The draws below stay inside these ranges and needn't reach their ends.
There are 2 independent parts, one for each index of `grp`. The reference program is written for one: setup_inputs(seed, part) draws one part's arguments, and reference() takes and returns one part's arrays. A program takes and returns all parts, laid end to end along the dimension named above; an argument that names none is the same for every part. Nothing has to cross between parts.
Inputs may be any that keep to these rules, and one draw needn't show every extreme that they name: context_pos holds each of 0 to 1535 once.
All inputs are finite; a program needn't handle non-finite values.
Results may differ from the reference program's by a relative error of at most 0.035.
Values may be sent and summed in bfloat16 or wider, within the bound.
A program may use at most 64 MiB of HBM per device.

```python
import math
import jax
import jax.numpy as jnp
from jax import lax

D = 2048
DH = 128
CONTEXT = 1536
LATENTS = 32


def drawn_rows(key, marker, count):
    noise = jnp.clip(jax.random.normal(jax.random.fold_in(key, marker), (count, D), jnp.float32), -4.0, 4.0)
    return noise


def drawn_matrix(key, marker, plain):
    base = jax.random.normal(jax.random.fold_in(key, marker), (D, D), jnp.float32) / math.sqrt(D)
    return jnp.clip(plain * base, -2.0, 2.0)


def draw_context(key, part):
    return drawn_rows(key, 7010, CONTEXT).astype(jnp.bfloat16)


def draw_latent_in(key, part):
    return drawn_rows(key, 7020, LATENTS).astype(jnp.bfloat16)


def draw_cross_q(key, part):
    return drawn_matrix(key, 7030, 4.0).astype(jnp.bfloat16)


def draw_cross_k(key, part):
    return drawn_matrix(key, 7040, 1.0).astype(jnp.bfloat16)


def draw_self_qkv(key, part):
    queries = drawn_matrix(key, 7050, 4.0)
    keys = drawn_matrix(key, 7060, 1.0)
    values = drawn_matrix(key, 7070, 1.0)
    return jnp.stack([queries, keys, values], axis=1).astype(jnp.bfloat16)


def level_of(own_key, extent, pieces, least, high):
    def one(axis_at, parts):
        steps = jax.random.uniform(jax.random.fold_in(jax.random.fold_in(own_key, 6), axis_at), (parts,), jnp.float32, least / len(pieces), high / len(pieces))
        return jnp.repeat(jnp.exp(steps), extent[axis_at] // parts).reshape((-1,) + (1,) * (len(extent) - axis_at - 1))

    loudness = one(*pieces[0])
    for cut in pieces[1:]:
        loudness = loudness * one(*cut)
    return loudness


def normal_values(stream_key, extent, spread, bound, cuts=(), held_as=jnp.bfloat16):
    values = jax.random.normal(stream_key, extent, jnp.float32) * spread
    if len(cuts) > 0:
        values = level_of(stream_key, extent, cuts, -0.22, 0.18) * values
    return jnp.clip(values, min=-bound, max=bound).astype(held_as)


def setup_inputs(seed: int = 0, part: int = 0) -> dict:
    splits = jax.random.split(jax.random.key(seed), 14)
    own_keys = jax.random.split(jax.random.fold_in(splits[13], part), 14)
    context = draw_context(jax.random.fold_in(jax.random.fold_in(splits[13], part), 71), part)
    context_pos = jax.random.permutation(own_keys[1], CONTEXT).astype(jnp.int32)
    latent_in = draw_latent_in(jax.random.fold_in(jax.random.fold_in(splits[13], part), 71), part)
    latent_start = jax.random.randint(own_keys[3], (1,), CONTEXT // 2, CONTEXT - LATENTS + 1).astype(jnp.int32)
    ctx_gain = jnp.clip(1.0 + 0.15 * jax.random.normal(splits[4], (D,), jnp.float32), 0.25, 1.75)
    lat_gain = jnp.clip(1.0 + 0.15 * jax.random.normal(splits[5], (D,), jnp.float32), 0.25, 1.75)
    mid_gain = jnp.clip(1.0 + 0.15 * jax.random.normal(splits[6], (D,), jnp.float32), 0.25, 1.75)
    cross_q = draw_cross_q(jax.random.fold_in(splits[13], 71), part)
    cross_k = draw_cross_k(jax.random.fold_in(splits[13], 71), part)
    cross_v = normal_values(splits[9], (D, D), D ** -0.5, 0.125, ((0, 4), (1, 4)))
    cross_out = normal_values(splits[10], (D, D), D ** -0.5, 0.125, ((0, 4), (1, 4)))
    self_qkv = draw_self_qkv(jax.random.fold_in(splits[13], 71), part)
    self_out = normal_values(splits[12], (D, D), D ** -0.5, 0.125, ((0, 4), (1, 4)))
    return dict(context=context, context_pos=context_pos, latent_in=latent_in, latent_start=latent_start, ctx_gain=ctx_gain, lat_gain=lat_gain, mid_gain=mid_gain, cross_q=cross_q, cross_k=cross_k, cross_v=cross_v, cross_out=cross_out, self_qkv=self_qkv, self_out=self_out)


EPS = 1e-05
NEG = -1e+30

def rms_rows(values, gain):
    wide = values.astype(jnp.float32)
    scale = lax.rsqrt(lax.optimization_barrier(jnp.mean(wide * wide, axis=-1, keepdims=True)) + EPS)
    return (wide * scale * gain).astype(jnp.bfloat16)

def contract_last(left, right):
    return lax.dot_general(left, right, (((1,), (1,)), ((), ())), preferred_element_type=jnp.float32)

def softmax_parts(queries, keys, values, allowed):
    heads = queries.shape[1] // DH
    maxima = []
    totals = []
    numerators = []
    for head in range(heads):
        begin = head * DH
        scores = contract_last(queries[:, begin:begin + DH], keys[:, begin:begin + DH]) * (1.0 / math.sqrt(DH))
        scores = jnp.where(allowed, scores, NEG)
        top = lax.optimization_barrier(jnp.max(scores, axis=1))
        weights = jnp.where(allowed, jnp.exp(scores - top[:, None]), 0.0)
        maxima.append(top)
        totals.append(lax.optimization_barrier(jnp.sum(weights, axis=1)))
        numerators.append(jnp.dot(weights.astype(jnp.bfloat16), values[:, begin:begin + DH], preferred_element_type=jnp.float32))
    return (jnp.stack(maxima, axis=1), jnp.stack(totals, axis=1), jnp.concatenate(numerators, axis=1))

def reference(context, context_pos, latent_in, latent_start, ctx_gain, lat_gain, mid_gain, cross_q, cross_k, cross_v, cross_out, self_qkv, self_out):
    normed_ctx = rms_rows(context, ctx_gain)
    keys = jnp.dot(normed_ctx, cross_k, preferred_element_type=jnp.float32).astype(jnp.bfloat16)
    values = jnp.dot(normed_ctx, cross_v, preferred_element_type=jnp.float32).astype(jnp.bfloat16)
    normed_lat = rms_rows(latent_in, lat_gain)
    queries = jnp.dot(normed_lat, cross_q, preferred_element_type=jnp.float32).astype(jnp.bfloat16)
    query_pos = latent_start[0] + jnp.arange(LATENTS, dtype=jnp.int32)
    allowed = context_pos[None, :] <= query_pos[:, None]
    unused, totals, numerators = softmax_parts(queries, keys, values, allowed)
    attended = (numerators / jnp.repeat(totals, DH, axis=1)).astype(jnp.bfloat16)
    hidden = (latent_in.astype(jnp.float32) + contract_last(attended, cross_out)).astype(jnp.bfloat16)
    normed_mid = rms_rows(hidden, mid_gain)
    projected = jnp.dot(normed_mid, self_qkv.reshape(D, 3 * D), preferred_element_type=jnp.float32)
    projected = projected.astype(jnp.bfloat16).reshape(LATENTS, 3, D)
    positions = jnp.arange(LATENTS, dtype=jnp.int32)
    causal = positions[None, :] <= positions[:, None]
    unused, self_totals, self_numerators = softmax_parts(projected[:, 0], projected[:, 1], projected[:, 2], causal)
    attended_self = (self_numerators / jnp.repeat(self_totals, DH, axis=1)).astype(jnp.bfloat16)
    return (hidden.astype(jnp.float32) + contract_last(attended_self, self_out)).astype(jnp.bfloat16)
```

```python
import math

import jax
import jax.numpy as jnp
from jax import lax
from jax.sharding import PartitionSpec as P

DH = 128


EPS = 1e-05
NEG = -1e30
HEADS_AXES = ("tp", "sub")


def contract_last(left, right):
    return lax.dot_general(
        left, right, (((1,), (1,)), ((), ())), preferred_element_type=jnp.float32
    )


def summed_over(partial, axis):
    everything = lax.all_gather(partial.astype(jnp.bfloat16), axis)
    return jnp.sum(everything.astype(jnp.float32), axis=0)


def on_device(
    context,
    context_pos,
    latent_in,
    latent_start,
    ctx_gain,
    lat_gain,
    mid_gain,
    cross_q,
    cross_k,
    cross_v,
    cross_out,
    self_qkv,
    self_out,
):
    rows, width = latent_in.shape
    depth, columns = cross_q.shape
    shards = lax.axis_size("ctx")
    heads = columns // DH
    latents = rows * shards
    own = lax.axis_index("ctx")
    mine = lambda array: lax.dynamic_slice_in_dim(array, own * depth, depth, array.ndim - 1)
    whole = lax.all_gather(context, HEADS_AXES, axis=1, tiled=True)
    all_latents = lax.all_gather(latent_in, "ctx", axis=0, tiled=True).astype(jnp.float32)
    lat_scale = lax.rsqrt(jnp.mean(all_latents * all_latents, axis=1, keepdims=True) + EPS)
    lat_part = mine(all_latents)
    normed_lat = (lat_part * lat_scale * mine(lat_gain)).astype(jnp.bfloat16)
    queries = summed_over(
        jnp.dot(normed_lat, cross_q, preferred_element_type=jnp.float32), "ctx"
    ).astype(jnp.bfloat16)
    split = [slice(head * DH, head * DH + DH) for head in range(heads)]
    absorbed = jnp.concatenate(
        [contract_last(queries[:, cut], cross_k[:, cut]) for cut in split], axis=0
    )
    absorbed = (absorbed * (mine(ctx_gain) * (1.0 / math.sqrt(DH)))).astype(jnp.bfloat16)
    absorbed = lax.all_gather(absorbed, "ctx", axis=1, tiled=True)

    wide = whole.astype(jnp.float32)
    token_scale = lax.rsqrt(jnp.mean(wide * wide, axis=1) + EPS)
    scores = contract_last(absorbed, whole) * token_scale[None, :]
    query_pos = latent_start[0] + jnp.arange(latents, dtype=jnp.int32)
    allowed = jnp.tile(context_pos[None, :] <= query_pos[:, None], (heads, 1))
    scores = jnp.where(allowed, scores, NEG)
    top = jnp.max(scores, axis=1, keepdims=True)
    weights = jnp.where(allowed, jnp.exp(scores - top), 0.0)
    total = jnp.sum(weights, axis=1, keepdims=True)
    mixed = jnp.dot(
        (weights * token_scale[None, :]).astype(jnp.bfloat16),
        whole,
        preferred_element_type=jnp.float32,
    ).astype(jnp.bfloat16)
    mixed = lax.all_to_all(
        mixed.reshape(heads * latents, shards, depth), "ctx", split_axis=1, concat_axis=0
    ).reshape(shards, heads * latents, depth)
    stats = lax.all_gather(jnp.concatenate([top, total], axis=1), "ctx")
    tops, totals = stats[:, :, :1], stats[:, :, 1:]
    factors = jnp.exp(tops - jnp.max(tops, axis=0))
    mixed = jnp.sum(mixed.astype(jnp.float32) * factors, axis=0) / jnp.sum(totals * factors, axis=0)
    mixed = (mixed * mine(ctx_gain)).astype(jnp.bfloat16)
    attended = jnp.concatenate(
        [
            jnp.dot(
                mixed[head * latents : (head + 1) * latents],
                cross_v[:, cut],
                preferred_element_type=jnp.float32,
            )
            for head, cut in enumerate(split)
        ],
        axis=1,
    )
    attended = summed_over(attended, "ctx").astype(jnp.bfloat16)
    cross_sum = summed_over(contract_last(attended, cross_out), HEADS_AXES)
    hidden = (lat_part + cross_sum).astype(jnp.bfloat16).astype(jnp.float32)
    squares = jnp.sum(lax.all_gather(jnp.sum(hidden * hidden, axis=1), "ctx"), axis=0)
    hidden_scale = lax.rsqrt(squares / width + EPS)
    projected = jnp.dot(
        (hidden * mine(mid_gain)).astype(jnp.bfloat16),
        self_qkv.reshape(depth, 3 * columns),
        preferred_element_type=jnp.float32,
    )
    projected = summed_over(projected, "ctx") * hidden_scale[:, None]
    projected = projected.astype(jnp.bfloat16).reshape(latents, 3, columns)
    index = jnp.arange(latents, dtype=jnp.int32)
    causal = index[None, :] <= index[:, None]
    parts = []
    for cut in split:
        scores = contract_last(projected[:, 0, cut], projected[:, 1, cut]) * (1.0 / math.sqrt(DH))
        scores = jnp.where(causal, scores, NEG)
        weights = jnp.where(causal, jnp.exp(scores - jnp.max(scores, axis=1, keepdims=True)), 0.0)
        numerator = jnp.dot(
            weights.astype(jnp.bfloat16), projected[:, 2, cut], preferred_element_type=jnp.float32
        )
        parts.append(numerator / jnp.sum(weights, axis=1, keepdims=True))
    attended_self = jnp.concatenate(parts, axis=1).astype(jnp.bfloat16)
    self_sum = summed_over(contract_last(attended_self, self_out), HEADS_AXES)
    result = (hidden + self_sum).astype(jnp.bfloat16)
    result = lax.all_to_all(
        result.reshape(shards, rows, depth), "ctx", split_axis=0, concat_axis=1
    ).reshape(rows, width)
    return lax.dynamic_slice_in_dim(result, lax.axis_index(HEADS_AXES) * columns, columns, 1)


def solution(mesh):
    return jax.shard_map(
        on_device,
        mesh=mesh,
        in_specs=(
            P(("grp", "ctx"), ("tp", "sub")),
            P(("grp", "ctx")),
            P(("grp", "ctx"), None),
            P("grp"),
            P(),
            P(),
            P(),
            P("ctx", ("tp", "sub")),
            P("ctx", ("tp", "sub")),
            P("ctx", ("tp", "sub")),
            P("ctx", ("tp", "sub")),
            P("ctx", None, ("tp", "sub")),
            P("ctx", ("tp", "sub")),
        ),
        out_specs=P(("grp", "ctx"), ("tp", "sub")),
        check_vma=False,
    )
```

```python
import math

import jax
import jax.numpy as jnp
from jax import lax
from jax.experimental import pallas as pl
from jax.experimental.pallas import tpu as pltpu
from jax.sharding import PartitionSpec as P

DH = 128


EPS = 1e-05
NEG = -1e30
HEADS_AXES = ("tp", "sub")
MESH = pl.DeviceIdType.MESH


def contract_last(left, right):
    return lax.dot_general(
        left, right, (((1,), (1,)), ((), ())), preferred_element_type=jnp.float32
    )


def summed_over(partial, axis):
    everything = lax.all_gather(partial.astype(jnp.bfloat16), axis)
    return jnp.sum(everything.astype(jnp.float32), axis=0)


def collectives(
    context,
    context_pos,
    latent_in,
    latent_start,
    ctx_gain,
    lat_gain,
    mid_gain,
    cross_q,
    cross_k,
    cross_v,
    cross_out,
    self_qkv,
    self_out,
):
    rows, width = latent_in.shape
    depth, columns = cross_q.shape
    shards = lax.axis_size("ctx")
    heads = columns // DH
    latents = rows * shards
    own = lax.axis_index("ctx")
    mine = lambda array: lax.dynamic_slice_in_dim(array, own * depth, depth, array.ndim - 1)
    whole = lax.all_gather(context, HEADS_AXES, axis=1, tiled=True)
    all_latents = lax.all_gather(latent_in, "ctx", axis=0, tiled=True).astype(jnp.float32)
    lat_scale = lax.rsqrt(jnp.mean(all_latents * all_latents, axis=1, keepdims=True) + EPS)
    lat_part = mine(all_latents)
    normed_lat = (lat_part * lat_scale * mine(lat_gain)).astype(jnp.bfloat16)
    queries = summed_over(
        jnp.dot(normed_lat, cross_q, preferred_element_type=jnp.float32), "ctx"
    ).astype(jnp.bfloat16)
    split = [slice(head * DH, head * DH + DH) for head in range(heads)]
    absorbed = jnp.concatenate(
        [contract_last(queries[:, cut], cross_k[:, cut]) for cut in split], axis=0
    )
    absorbed = (absorbed * (mine(ctx_gain) * (1.0 / math.sqrt(DH)))).astype(jnp.bfloat16)
    absorbed = lax.all_gather(absorbed, "ctx", axis=1, tiled=True)

    wide = whole.astype(jnp.float32)
    token_scale = lax.rsqrt(jnp.mean(wide * wide, axis=1) + EPS)
    scores = contract_last(absorbed, whole) * token_scale[None, :]
    query_pos = latent_start[0] + jnp.arange(latents, dtype=jnp.int32)
    allowed = jnp.tile(context_pos[None, :] <= query_pos[:, None], (heads, 1))
    scores = jnp.where(allowed, scores, NEG)
    top = jnp.max(scores, axis=1, keepdims=True)
    weights = jnp.where(allowed, jnp.exp(scores - top), 0.0)
    total = jnp.sum(weights, axis=1, keepdims=True)
    mixed = jnp.dot(
        (weights * token_scale[None, :]).astype(jnp.bfloat16),
        whole,
        preferred_element_type=jnp.float32,
    ).astype(jnp.bfloat16)
    mixed = lax.all_to_all(
        mixed.reshape(heads * latents, shards, depth), "ctx", split_axis=1, concat_axis=0
    ).reshape(shards, heads * latents, depth)
    stats = lax.all_gather(jnp.concatenate([top, total], axis=1), "ctx")
    tops, totals = stats[:, :, :1], stats[:, :, 1:]
    factors = jnp.exp(tops - jnp.max(tops, axis=0))
    mixed = jnp.sum(mixed.astype(jnp.float32) * factors, axis=0) / jnp.sum(totals * factors, axis=0)
    mixed = (mixed * mine(ctx_gain)).astype(jnp.bfloat16)
    attended = jnp.concatenate(
        [
            jnp.dot(
                mixed[head * latents : (head + 1) * latents],
                cross_v[:, cut],
                preferred_element_type=jnp.float32,
            )
            for head, cut in enumerate(split)
        ],
        axis=1,
    )
    attended = summed_over(attended, "ctx").astype(jnp.bfloat16)
    cross_sum = summed_over(contract_last(attended, cross_out), HEADS_AXES)
    hidden = (lat_part + cross_sum).astype(jnp.bfloat16).astype(jnp.float32)
    squares = jnp.sum(lax.all_gather(jnp.sum(hidden * hidden, axis=1), "ctx"), axis=0)
    hidden_scale = lax.rsqrt(squares / width + EPS)
    projected = jnp.dot(
        (hidden * mine(mid_gain)).astype(jnp.bfloat16),
        self_qkv.reshape(depth, 3 * columns),
        preferred_element_type=jnp.float32,
    )
    projected = summed_over(projected, "ctx") * hidden_scale[:, None]
    projected = projected.astype(jnp.bfloat16).reshape(latents, 3, columns)
    index = jnp.arange(latents, dtype=jnp.int32)
    causal = index[None, :] <= index[:, None]
    parts = []
    for cut in split:
        scores = contract_last(projected[:, 0, cut], projected[:, 1, cut]) * (1.0 / math.sqrt(DH))
        scores = jnp.where(causal, scores, NEG)
        weights = jnp.where(causal, jnp.exp(scores - jnp.max(scores, axis=1, keepdims=True)), 0.0)
        numerator = jnp.dot(
            weights.astype(jnp.bfloat16), projected[:, 2, cut], preferred_element_type=jnp.float32
        )
        parts.append(numerator / jnp.sum(weights, axis=1, keepdims=True))
    attended_self = jnp.concatenate(parts, axis=1).astype(jnp.bfloat16)
    self_sum = summed_over(contract_last(attended_self, self_out), HEADS_AXES)
    result = (hidden + self_sum).astype(jnp.bfloat16)
    result = lax.all_to_all(
        result.reshape(shards, rows, depth), "ctx", split_axis=0, concat_axis=1
    ).reshape(rows, width)
    return lax.dynamic_slice_in_dim(result, lax.axis_index(HEADS_AXES) * columns, columns, 1)


def step_kernel(
    start_ref,
    pos_ref,
    latent_ref,
    gain_ref,
    context_ref,
    q_hbm,
    k_hbm,
    v_hbm,
    out_hbm,
    qkv_hbm,
    last_hbm,
    result_ref,
    ctx_buf,
    q_ref,
    k_ref,
    v_ref,
    o_ref,
    qkv_ref,
    last_ref,
    lat_stage,
    lat_buf,
    query_stage,
    query_buf,
    absorbed_buf,
    stat_stage,
    stat_buf,
    mixed_stage,
    mixed_buf,
    att_stage,
    att_buf,
    cross_stage,
    cross_buf,
    proj_stage,
    proj_buf,
    square_stage,
    square_buf,
    end_stage,
    end_buf,
    load_sem,
    ring_send,
    ring_recv,
    ctx_send,
    ctx_recv,
    cross_send,
    cross_recv,
    end_send,
    end_recv,
):
    shards, tps, subs = lax.axis_size("ctx"), lax.axis_size("tp"), lax.axis_size("sub")
    peers = tps * subs
    own, tp, sub = lax.axis_index("ctx"), lax.axis_index("tp"), lax.axis_index("sub")
    spot = tp * subs + sub
    rows, width = latent_ref.shape
    depth, columns = q_ref.shape
    heads = columns // DH
    latents = rows * shards
    tokens = context_ref.shape[0]
    ratio = columns // depth
    f32, bf16 = jnp.float32, jnp.bfloat16
    split = [slice(head * DH, head * DH + DH) for head in range(heads)]

    loads = [
        pltpu.make_async_copy(source, target, load_sem.at[index])
        for index, (source, target) in enumerate(
            (
                (context_ref, ctx_buf.at[spot]),
                (q_hbm, q_ref),
                (k_hbm, k_ref),
                (v_hbm, v_ref),
                (out_hbm, o_ref),
                (qkv_hbm, qkv_ref),
                (last_hbm, last_ref),
            )
        )
    ]
    for load in loads:
        load.start()

    barrier = pltpu.get_barrier_semaphore()
    everyone = shards * peers
    me = own * peers + spot
    for step in range(1, everyone):
        other = lax.rem(me + step, everyone)
        pl.semaphore_signal(
            barrier,
            inc=1,
            device_id={
                "ctx": other // peers,
                "tp": lax.rem(other, peers) // subs,
                "sub": lax.rem(other, subs),
            },
            device_id_type=MESH,
        )

    wide = latent_ref[...].astype(f32)
    scale = lax.rsqrt(jnp.mean(wide * wide, axis=1, keepdims=True) + EPS)
    for shard in range(shards):
        part = wide[:, shard * depth : (shard + 1) * depth]
        lat_stage[shard] = jnp.concatenate(
            [part, part * scale * gain_ref[1, shard]], axis=0
        ).astype(bf16)
    pl.semaphore_wait(barrier, everyone - 1)

    started = []

    def send(source, target, send_sem, recv_sem, device):
        copy = pltpu.make_async_remote_copy(
            src_ref=source,
            dst_ref=target,
            send_sem=send_sem,
            recv_sem=recv_sem,
            device_id=device,
            device_id_type=MESH,
        )
        copy.start()
        started.append(copy)
        return copy

    def ring(phase, pick, target):
        return [
            send(
                pick(lax.rem(own + step, shards)),
                target(step),
                ring_send.at[phase, step],
                ring_recv.at[phase, step],
                {"ctx": lax.rem(own + step, shards)},
            )
            for step in range(1, shards)
        ]

    def arrive(copies):
        for copy in copies:
            copy.wait_recv()

    def summed(first, buf):
        for step in range(1, buf.shape[0]):
            first = first + buf[step].astype(f32)
        return first

    moved = ring(0, lambda peer: lat_stage.at[peer], lambda step: lat_buf.at[own])
    across = [
        send(
            context_ref,
            ctx_buf.at[spot],
            ctx_send.at[0, step],
            ctx_recv.at[0, step],
            {"tp": lax.rem(tp + step, tps)},
        )
        for step in range(1, tps)
    ]
    beside = [
        send(
            context_ref,
            ctx_buf.at[spot],
            ctx_send.at[tps, step],
            ctx_recv.at[tps, step],
            {"sub": lax.rem(sub + step, subs)},
        )
        for step in range(1, subs)
    ]
    lat_buf[own] = lat_stage[own]
    loads[1].wait()
    arrive(moved)
    blocks = [lat_buf[shard].astype(f32) for shard in range(shards)]
    lat_part = jnp.concatenate([block[:rows] for block in blocks], axis=0)
    normed = jnp.concatenate([block[rows:] for block in blocks], axis=0).astype(bf16)
    partial = jnp.dot(normed, q_ref[...], preferred_element_type=f32)
    query_stage[...] = partial.astype(bf16)
    moved = ring(1, lambda peer: query_stage, lambda step: query_buf.at[step])
    loads[2].wait()
    arrive(moved)
    queries = summed(partial, query_buf).astype(bf16)
    absorbed = jnp.concatenate(
        [contract_last(queries[:, cut], k_ref[:, cut]) for cut in split], axis=0
    )
    absorbed_buf[own] = (absorbed * (gain_ref[0, own] * (1.0 / math.sqrt(DH)))).astype(bf16)
    moved = ring(2, lambda peer: absorbed_buf.at[own], lambda step: absorbed_buf.at[own])

    for step, copy in enumerate(across, 1):
        copy.wait_recv()
        block = lax.rem(tp + tps - step, tps) * subs + sub
        beside = beside + [
            send(
                ctx_buf.at[block],
                ctx_buf.at[block],
                ctx_send.at[step, hop],
                ctx_recv.at[step, hop],
                {"sub": lax.rem(sub + hop, subs)},
            )
            for hop in range(1, subs)
        ]
    loads[0].wait()
    arrive(beside)
    squares = jnp.zeros((8, tokens), f32)
    for block in range(peers):
        wide = ctx_buf[block].astype(f32)
        squares = squares + lax.dot_general(
            jnp.ones((8, columns), f32),
            wide * wide,
            (((1,), (1,)), ((), ())),
            precision=lax.Precision.HIGHEST,
            preferred_element_type=f32,
        )
    token_scale = lax.rsqrt(squares[:1] / width + EPS)
    query_pos = start_ref[0] + lax.broadcasted_iota(jnp.int32, (latents, tokens), 0)
    query_pos = jnp.concatenate([query_pos] * heads, axis=0)
    allowed = jnp.broadcast_to(pos_ref[...], query_pos.shape) <= query_pos
    arrive(moved)

    def features(shard):
        inside = shard % ratio * depth
        return ctx_buf[shard // ratio][:, inside : inside + depth]

    scores = contract_last(absorbed_buf[0], features(0))
    for shard in range(1, shards):
        scores = scores + contract_last(absorbed_buf[shard], features(shard))
    scores = jnp.where(allowed, scores * token_scale, NEG)
    top = jnp.max(scores, axis=1, keepdims=True)
    weights = jnp.where(allowed, jnp.exp(scores - top), 0.0)
    total = jnp.sum(weights, axis=1, keepdims=True)
    lane = lax.broadcasted_iota(jnp.int32, (heads * latents, 128), 1)
    stat_stage[...] = jnp.transpose(jnp.where(lane == 0, top, total))[:8]
    moved = ring(3, lambda peer: stat_stage, lambda step: stat_buf.at[step])
    scaled = (weights * token_scale).astype(bf16)
    for shard in range(shards):
        mixed_stage[shard] = jnp.dot(
            scaled, features(shard), preferred_element_type=f32
        ).astype(bf16)
    moved = moved + ring(4, lambda peer: mixed_stage.at[peer], lambda step: mixed_buf.at[step])
    stat_buf[0] = stat_stage[...]
    mixed_buf[0] = mixed_stage[own]
    loads[3].wait()
    arrive(moved)
    tops = jnp.concatenate([stat_buf[step][0:1] for step in range(shards)], axis=0)
    totals = jnp.concatenate([stat_buf[step][1:2] for step in range(shards)], axis=0)
    factors = jnp.exp(tops - jnp.max(tops, axis=0, keepdims=True))
    factors = factors / jnp.sum(totals * factors, axis=0, keepdims=True)
    short = -shards % 128
    factors = jnp.transpose(
        jnp.concatenate([factors, jnp.zeros((short, factors.shape[1]), f32)], axis=0)
    )
    mixed = mixed_buf[0].astype(f32) * factors[:, 0:1]
    for step in range(1, shards):
        mixed = mixed + mixed_buf[step].astype(f32) * factors[:, step : step + 1]
    mixed = (mixed * gain_ref[0, own]).astype(bf16)
    partial = jnp.concatenate(
        [
            jnp.dot(
                mixed[head * latents : (head + 1) * latents],
                v_ref[:, cut],
                preferred_element_type=f32,
            )
            for head, cut in enumerate(split)
        ],
        axis=1,
    )
    att_stage[...] = partial.astype(bf16)
    moved = ring(5, lambda peer: att_stage, lambda step: att_buf.at[step])
    loads[4].wait()
    arrive(moved)
    attended = summed(partial, att_buf).astype(bf16)
    partial = contract_last(attended, o_ref[...])
    cross_stage[...] = partial.astype(bf16)
    moved = []
    for step in range(1, peers):
        other = lax.rem(spot + step, peers)
        moved.append(
            send(
                cross_stage,
                cross_buf.at[step],
                cross_send.at[step],
                cross_recv.at[step],
                {"tp": other // subs, "sub": lax.rem(other, subs)},
            )
        )
    loads[5].wait()
    arrive(moved)
    hidden = (lat_part + summed(partial, cross_buf)).astype(bf16).astype(f32)
    scaled = (hidden * gain_ref[2, own]).astype(bf16)
    partials = [
        jnp.dot(scaled, qkv_ref[index], preferred_element_type=f32) for index in range(3)
    ]
    partial = jnp.concatenate(partials, axis=1)
    proj_stage[...] = partial.astype(bf16)
    square = jnp.broadcast_to(
        jnp.sum(hidden * hidden, axis=1, keepdims=True), square_stage.shape
    )
    square_stage[...] = square
    moved = ring(6, lambda peer: square_stage, lambda step: square_buf.at[step])
    moved = moved + ring(7, lambda peer: proj_stage, lambda step: proj_buf.at[step])
    loads[6].wait()
    arrive(moved)
    hidden_scale = lax.rsqrt(summed(square, square_buf)[:, :1] / width + EPS)
    projected = (summed(partial, proj_buf) * hidden_scale).astype(bf16)
    causal = lax.broadcasted_iota(jnp.int32, (latents, latents), 1) <= lax.broadcasted_iota(
        jnp.int32, (latents, latents), 0
    )
    parts = []
    for head in range(heads):
        self_q, self_k, self_v = (
            projected[:, at * columns + head * DH : at * columns + (head + 1) * DH]
            for at in range(3)
        )
        scores = contract_last(self_q, self_k) * (1.0 / math.sqrt(DH))
        scores = jnp.where(causal, scores, NEG)
        weights = jnp.where(causal, jnp.exp(scores - jnp.max(scores, axis=1, keepdims=True)), 0.0)
        numerator = jnp.dot(weights.astype(bf16), self_v, preferred_element_type=f32)
        parts.append(numerator / jnp.sum(weights, axis=1, keepdims=True))
    attended = jnp.concatenate(parts, axis=1).astype(bf16)
    partial = contract_last(attended, last_ref[...])
    partial = partial + hidden * jnp.where(spot == 0, 1.0, 0.0).astype(f32)

    goal = own // ratio
    slot = lax.rem(own, ratio) * peers + spot
    for shard in range(shards):
        end_stage[shard] = partial[shard * rows : (shard + 1) * rows]

    def hand(step):
        other = lax.rem(own + step, shards)
        return pltpu.make_async_remote_copy(
            src_ref=end_stage.at[other],
            dst_ref=end_buf.at[slot],
            send_sem=end_send.at[step],
            recv_sem=end_recv.at[slot],
            device_id={"ctx": other, "tp": goal // subs, "sub": lax.rem(goal, subs)},
            device_id_type=MESH,
        )

    for step in range(1, shards):
        hand(step).start()

    @pl.when(goal != spot)
    def _():
        hand(0).start()

    @pl.when(goal == spot)
    def _():
        end_buf[slot] = end_stage[own]

    for inside in range(ratio):
        for source in range(peers):
            at = inside * peers + source

            @pl.when(jnp.logical_or(spot * ratio + inside != own, spot != source))
            def _():
                pltpu.make_async_remote_copy(
                    src_ref=end_stage.at[0],
                    dst_ref=end_buf.at[at],
                    send_sem=end_send.at[0],
                    recv_sem=end_recv.at[at],
                    device_id={"ctx": lax.rem(own + 1, shards)},
                    device_id_type=MESH,
                ).wait_recv()

    for inside in range(ratio):
        first = end_buf[inside * peers]
        for source in range(1, peers):
            first = first + end_buf[inside * peers + source]
        result_ref[:, inside * depth : (inside + 1) * depth] = first.astype(bf16)
    for copy in started:
        copy.wait_send()
    for step in range(1, shards):
        hand(step).wait_send()

    @pl.when(goal != spot)
    def _():
        hand(0).wait_send()


def fused(
    context,
    context_pos,
    latent_in,
    latent_start,
    ctx_gain,
    lat_gain,
    mid_gain,
    cross_q,
    cross_k,
    cross_v,
    cross_out,
    self_qkv,
    self_out,
):
    rows, width = latent_in.shape
    depth, columns = cross_q.shape
    tokens = context.shape[0]
    shards, tps, subs = lax.axis_size("ctx"), lax.axis_size("tp"), lax.axis_size("sub")
    peers = tps * subs
    latents = rows * shards
    lines = columns // DH * latents
    ends = columns // depth * peers
    gains = jnp.stack([ctx_gain, lat_gain, mid_gain]).reshape(3, shards, 1, depth)
    f32, bf16 = jnp.float32, jnp.bfloat16
    vmem, dma = pltpu.VMEM, pltpu.SemaphoreType.DMA
    held = pl.BlockSpec(memory_space=pltpu.VMEM)
    away = pl.BlockSpec(memory_space=pl.ANY)
    return pl.pallas_call(
        step_kernel,
        out_shape=jax.ShapeDtypeStruct((rows, columns), bf16),
        in_specs=[pl.BlockSpec(memory_space=pltpu.SMEM)] + [held] * 3 + [away] * 7,
        out_specs=held,
        scratch_shapes=[
            vmem((peers, tokens, columns), bf16),
            vmem((depth, columns), bf16),
            vmem((depth, columns), bf16),
            vmem((depth, columns), bf16),
            vmem((depth, columns), bf16),
            vmem((3, depth, columns), bf16),
            vmem((depth, columns), bf16),
            vmem((shards, 2 * rows, depth), bf16),
            vmem((shards, 2 * rows, depth), bf16),
            vmem((latents, columns), bf16),
            vmem((shards, latents, columns), bf16),
            vmem((shards, lines, depth), bf16),
            vmem((8, lines), f32),
            vmem((shards, 8, lines), f32),
            vmem((shards, lines, depth), bf16),
            vmem((shards, lines, depth), bf16),
            vmem((latents, columns), bf16),
            vmem((shards, latents, columns), bf16),
            vmem((latents, depth), bf16),
            vmem((peers, latents, depth), bf16),
            vmem((latents, 3 * columns), bf16),
            vmem((shards, latents, 3 * columns), bf16),
            vmem((latents, 128), f32),
            vmem((shards, latents, 128), f32),
            vmem((shards, rows, depth), f32),
            vmem((ends, rows, depth), f32),
            dma((7,)),
            dma((8, shards)),
            dma((8, shards)),
            dma((tps + 1, max(tps, subs))),
            dma((tps + 1, max(tps, subs))),
            dma((peers,)),
            dma((peers,)),
            dma((shards,)),
            dma((ends,)),
        ],
        compiler_params=pltpu.CompilerParams(
            collective_id=0, has_side_effects=True, vmem_limit_bytes=56 << 20
        ),
    )(
        latent_start,
        context_pos.reshape(1, tokens),
        latent_in,
        gains,
        context,
        cross_q,
        cross_k,
        cross_v,
        cross_out,
        jnp.transpose(self_qkv, (1, 0, 2)),
        self_out,
    )


def on_device(*arrays):
    depth, columns = arrays[7].shape
    if depth % 128 == 0 and columns % depth == 0:
        return fused(*arrays)
    return collectives(*arrays)


def solution(mesh):
    return jax.shard_map(
        on_device,
        mesh=mesh,
        in_specs=(
            P(("grp", "ctx"), ("tp", "sub")),
            P(("grp", "ctx")),
            P(("grp", "ctx"), None),
            P("grp"),
            P(),
            P(),
            P(),
            P("ctx", ("tp", "sub")),
            P("ctx", ("tp", "sub")),
            P("ctx", ("tp", "sub")),
            P("ctx", ("tp", "sub")),
            P("ctx", None, ("tp", "sub")),
            P("ctx", ("tp", "sub")),
        ),
        out_specs=P(("grp", "ctx"), ("tp", "sub")),
        check_vma=False,
    )
```

```python
import math

import jax
import jax.numpy as jnp
from jax import lax
from jax.experimental import pallas as pl
from jax.experimental.pallas import tpu as pltpu
from jax.sharding import PartitionSpec as P

DH = 128


EPS = 1e-05
NEG = -1e30
HEADS_AXES = ("tp", "sub")
MESH = pl.DeviceIdType.MESH
CHUNKS = 4


def contract_last(left, right):
    return lax.dot_general(
        left, right, (((1,), (1,)), ((), ())), preferred_element_type=jnp.float32
    )


def summed_over(partial, axis):
    everything = lax.all_gather(partial.astype(jnp.bfloat16), axis)
    return jnp.sum(everything.astype(jnp.float32), axis=0)


def collectives(
    context,
    context_pos,
    latent_in,
    latent_start,
    ctx_gain,
    lat_gain,
    mid_gain,
    cross_q,
    cross_k,
    cross_v,
    cross_out,
    self_qkv,
    self_out,
):
    rows, width = latent_in.shape
    depth, columns = cross_q.shape
    shards = lax.axis_size("ctx")
    heads = columns // DH
    latents = rows * shards
    own = lax.axis_index("ctx")
    mine = lambda array: lax.dynamic_slice_in_dim(array, own * depth, depth, array.ndim - 1)
    whole = lax.all_gather(context, HEADS_AXES, axis=1, tiled=True)
    all_latents = lax.all_gather(latent_in, "ctx", axis=0, tiled=True).astype(jnp.float32)
    lat_scale = lax.rsqrt(jnp.mean(all_latents * all_latents, axis=1, keepdims=True) + EPS)
    lat_part = mine(all_latents)
    normed_lat = (lat_part * lat_scale * mine(lat_gain)).astype(jnp.bfloat16)
    queries = summed_over(
        jnp.dot(normed_lat, cross_q, preferred_element_type=jnp.float32), "ctx"
    ).astype(jnp.bfloat16)
    split = [slice(head * DH, head * DH + DH) for head in range(heads)]
    absorbed = jnp.concatenate(
        [contract_last(queries[:, cut], cross_k[:, cut]) for cut in split], axis=0
    )
    absorbed = (absorbed * (mine(ctx_gain) * (1.0 / math.sqrt(DH)))).astype(jnp.bfloat16)
    absorbed = lax.all_gather(absorbed, "ctx", axis=1, tiled=True)

    wide = whole.astype(jnp.float32)
    token_scale = lax.rsqrt(jnp.mean(wide * wide, axis=1) + EPS)
    scores = contract_last(absorbed, whole) * token_scale[None, :]
    query_pos = latent_start[0] + jnp.arange(latents, dtype=jnp.int32)
    allowed = jnp.tile(context_pos[None, :] <= query_pos[:, None], (heads, 1))
    scores = jnp.where(allowed, scores, NEG)
    top = jnp.max(scores, axis=1, keepdims=True)
    weights = jnp.where(allowed, jnp.exp(scores - top), 0.0)
    total = jnp.sum(weights, axis=1, keepdims=True)
    mixed = jnp.dot(
        (weights * token_scale[None, :]).astype(jnp.bfloat16),
        whole,
        preferred_element_type=jnp.float32,
    ).astype(jnp.bfloat16)
    mixed = lax.all_to_all(
        mixed.reshape(heads * latents, shards, depth), "ctx", split_axis=1, concat_axis=0
    ).reshape(shards, heads * latents, depth)
    stats = lax.all_gather(jnp.concatenate([top, total], axis=1), "ctx")
    tops, totals = stats[:, :, :1], stats[:, :, 1:]
    factors = jnp.exp(tops - jnp.max(tops, axis=0))
    mixed = jnp.sum(mixed.astype(jnp.float32) * factors, axis=0) / jnp.sum(totals * factors, axis=0)
    mixed = (mixed * mine(ctx_gain)).astype(jnp.bfloat16)
    attended = jnp.concatenate(
        [
            jnp.dot(
                mixed[head * latents : (head + 1) * latents],
                cross_v[:, cut],
                preferred_element_type=jnp.float32,
            )
            for head, cut in enumerate(split)
        ],
        axis=1,
    )
    attended = summed_over(attended, "ctx").astype(jnp.bfloat16)
    cross_sum = summed_over(contract_last(attended, cross_out), HEADS_AXES)
    hidden = (lat_part + cross_sum).astype(jnp.bfloat16).astype(jnp.float32)
    squares = jnp.sum(lax.all_gather(jnp.sum(hidden * hidden, axis=1), "ctx"), axis=0)
    hidden_scale = lax.rsqrt(squares / width + EPS)
    projected = jnp.dot(
        (hidden * mine(mid_gain)).astype(jnp.bfloat16),
        self_qkv.reshape(depth, 3 * columns),
        preferred_element_type=jnp.float32,
    )
    projected = summed_over(projected, "ctx") * hidden_scale[:, None]
    projected = projected.astype(jnp.bfloat16).reshape(latents, 3, columns)
    index = jnp.arange(latents, dtype=jnp.int32)
    causal = index[None, :] <= index[:, None]
    parts = []
    for cut in split:
        scores = contract_last(projected[:, 0, cut], projected[:, 1, cut]) * (1.0 / math.sqrt(DH))
        scores = jnp.where(causal, scores, NEG)
        weights = jnp.where(causal, jnp.exp(scores - jnp.max(scores, axis=1, keepdims=True)), 0.0)
        numerator = jnp.dot(
            weights.astype(jnp.bfloat16), projected[:, 2, cut], preferred_element_type=jnp.float32
        )
        parts.append(numerator / jnp.sum(weights, axis=1, keepdims=True))
    attended_self = jnp.concatenate(parts, axis=1).astype(jnp.bfloat16)
    self_sum = summed_over(contract_last(attended_self, self_out), HEADS_AXES)
    result = (hidden + self_sum).astype(jnp.bfloat16)
    result = lax.all_to_all(
        result.reshape(shards, rows, depth), "ctx", split_axis=0, concat_axis=1
    ).reshape(rows, width)
    return lax.dynamic_slice_in_dim(result, lax.axis_index(HEADS_AXES) * columns, columns, 1)


def step_kernel(
    start_ref,
    pos_ref,
    latent_ref,
    ctx_gain_ref,
    lat_gain_ref,
    mid_gain_ref,
    context_ref,
    q_hbm,
    k_hbm,
    v_hbm,
    out_hbm,
    qkv_hbm,
    last_hbm,
    result_ref,
    ctx_buf,
    q_ref,
    k_ref,
    v_ref,
    o_ref,
    qkv_ref,
    last_ref,
    lat_stage,
    lat_buf,
    query_stage,
    query_buf,
    absorbed_buf,
    stat_stage,
    stat_buf,
    mixed_stage,
    mixed_buf,
    att_stage,
    att_buf,
    cross_stage,
    cross_buf,
    proj_stage,
    proj_buf,
    self_buf,
    end_stage,
    end_buf,
    load_sem,
    ring_send,
    ring_recv,
    ctx_send,
    ctx_recv,
    cross_send,
    cross_recv,
    end_send,
    end_recv,
):
    shards, tps, subs = lax.axis_size("ctx"), lax.axis_size("tp"), lax.axis_size("sub")
    peers = tps * subs
    own, tp, sub = lax.axis_index("ctx"), lax.axis_index("tp"), lax.axis_index("sub")
    spot = tp * subs + sub
    rows, width = latent_ref.shape
    depth, columns = q_ref.shape
    heads = columns // DH
    latents = rows * shards
    tokens = context_ref.shape[0]
    ratio = columns // depth
    f32, bf16 = jnp.float32, jnp.bfloat16
    split = [slice(head * DH, head * DH + DH) for head in range(heads)]

    loads = [
        pltpu.make_async_copy(source, target, load_sem.at[index])
        for index, (source, target) in enumerate(
            (
                (context_ref, ctx_buf.at[spot]),
                (q_hbm, q_ref),
                (k_hbm, k_ref),
                (v_hbm, v_ref),
                (out_hbm, o_ref),
                (qkv_hbm, qkv_ref),
                (last_hbm, last_ref),
            )
        )
    ]
    for load in loads:
        load.start()

    barrier = pltpu.get_barrier_semaphore()
    everyone = shards * peers
    me = own * peers + spot
    for step in range(1, everyone):
        other = lax.rem(me + step, everyone)
        pl.semaphore_signal(
            barrier,
            inc=1,
            device_id={
                "ctx": other // peers,
                "tp": lax.rem(other, peers) // subs,
                "sub": lax.rem(other, subs),
            },
            device_id_type=MESH,
        )

    wide = latent_ref[...].astype(f32)
    scale = lax.rsqrt(jnp.mean(wide * wide, axis=1, keepdims=True) + EPS)
    for shard in range(shards):
        part = wide[:, shard * depth : (shard + 1) * depth]
        lat_stage[shard] = jnp.concatenate(
            [part, part * scale * lat_gain_ref[shard]], axis=0
        ).astype(bf16)
    pl.semaphore_wait(barrier, everyone - 1)

    started = []

    def send(source, target, send_sem, recv_sem, device):
        copy = pltpu.make_async_remote_copy(
            src_ref=source,
            dst_ref=target,
            send_sem=send_sem,
            recv_sem=recv_sem,
            device_id=device,
            device_id_type=MESH,
        )
        copy.start()
        started.append(copy)
        return copy

    def ring(phase, pick, target):
        return [
            send(
                pick(lax.rem(own + step, shards)),
                target(step),
                ring_send.at[phase, step],
                ring_recv.at[phase, step],
                {"ctx": lax.rem(own + step, shards)},
            )
            for step in range(1, shards)
        ]

    def arrive(copies):
        for copy in copies:
            copy.wait_recv()

    def summed(first, buf):
        for step in range(1, buf.shape[0]):
            first = first + buf[step].astype(f32)
        return first

    moved = ring(0, lambda peer: lat_stage.at[peer], lambda step: lat_buf.at[own])
    chunk = tokens // CHUNKS
    pieces = [pl.ds(piece * chunk, chunk) for piece in range(CHUNKS)]
    across = [
        [
            send(
                context_ref.at[piece],
                ctx_buf.at[spot, piece],
                ctx_send.at[0, step, at],
                ctx_recv.at[0, step, at],
                {"tp": lax.rem(tp + step, tps)},
            )
            for step in range(1, tps)
        ]
        for at, piece in enumerate(pieces)
    ]
    beside = [
        send(
            context_ref,
            ctx_buf.at[spot],
            ctx_send.at[tps, step, 0],
            ctx_recv.at[tps, step, 0],
            {"sub": lax.rem(sub + step, subs)},
        )
        for step in range(1, subs)
    ]

    def forward(at):
        handed = []
        for step, copy in enumerate(across[at], 1):
            copy.wait_recv()
            block = lax.rem(tp + tps - step, tps) * subs + sub
            handed = handed + [
                send(
                    ctx_buf.at[block, pieces[at]],
                    ctx_buf.at[block, pieces[at]],
                    ctx_send.at[step, hop, at],
                    ctx_recv.at[step, hop, at],
                    {"sub": lax.rem(sub + hop, subs)},
                )
                for hop in range(1, subs)
            ]
        return handed

    lat_buf[own] = lat_stage[own]
    loads[1].wait()
    arrive(moved)
    blocks = [lat_buf[shard].astype(f32) for shard in range(shards)]
    lat_part = jnp.concatenate([block[:rows] for block in blocks], axis=0)
    normed = jnp.concatenate([block[rows:] for block in blocks], axis=0).astype(bf16)
    partial = jnp.dot(normed, q_ref[...], preferred_element_type=f32)
    query_stage[...] = partial.astype(bf16)
    moved = ring(1, lambda peer: query_stage, lambda step: query_buf.at[step])
    beside = beside + forward(0)
    loads[2].wait()
    arrive(moved)
    beside = beside + forward(1)
    queries = summed(partial, query_buf).astype(bf16)
    absorbed = jnp.concatenate(
        [contract_last(queries[:, cut], k_ref[:, cut]) for cut in split], axis=0
    )
    absorbed_buf[own] = (absorbed * (ctx_gain_ref[own] * (1.0 / math.sqrt(DH)))).astype(bf16)
    moved = ring(2, lambda peer: absorbed_buf.at[own], lambda step: absorbed_buf.at[own])

    for at in range(2, CHUNKS):
        beside = beside + forward(at)
    loads[0].wait()
    arrive(beside)
    squares = jnp.zeros((8, tokens), f32)
    for block in range(peers):
        wide = ctx_buf[block].astype(f32)
        squares = squares + lax.dot_general(
            jnp.ones((8, columns), f32),
            wide * wide,
            (((1,), (1,)), ((), ())),
            precision=lax.Precision.HIGHEST,
            preferred_element_type=f32,
        )
    token_scale = lax.rsqrt(squares[:1] / width + EPS)
    query_pos = start_ref[0] + lax.broadcasted_iota(jnp.int32, (latents, tokens), 0)
    query_pos = jnp.concatenate([query_pos] * heads, axis=0)
    allowed = jnp.broadcast_to(pos_ref[...].reshape(1, tokens), query_pos.shape) <= query_pos
    scores = contract_last(absorbed_buf[own], ctx_buf[own])
    for step, copy in enumerate(moved, 1):
        copy.wait_recv()
        source = lax.rem(own + shards - step, shards)
        scores = scores + contract_last(absorbed_buf[source], ctx_buf[source])
    scores = jnp.where(allowed, scores * token_scale, NEG)
    top = jnp.max(scores, axis=1, keepdims=True)
    weights = jnp.where(allowed, jnp.exp(scores - top), 0.0)
    total = jnp.sum(weights, axis=1, keepdims=True)
    lane = lax.broadcasted_iota(jnp.int32, (heads * latents, 128), 1)
    stat_stage[...] = jnp.transpose(jnp.where(lane == 0, top, total))[:8]
    moved = ring(3, lambda peer: stat_stage, lambda step: stat_buf.at[step])
    scaled = (weights * token_scale).astype(bf16)
    mixing = []
    for step in range(1, shards):
        other = lax.rem(own + step, shards)
        mixed_stage[step] = jnp.dot(
            scaled, ctx_buf[other], preferred_element_type=f32
        ).astype(bf16)
        mixing.append(
            send(
                mixed_stage.at[step],
                mixed_buf.at[step],
                ring_send.at[4, step],
                ring_recv.at[4, step],
                {"ctx": other},
            )
        )
    mixed = jnp.dot(scaled, ctx_buf[own], preferred_element_type=f32)
    stat_buf[0] = stat_stage[...]
    loads[3].wait()
    arrive(moved)
    tops = jnp.concatenate([stat_buf[step][0:1] for step in range(shards)], axis=0)
    totals = jnp.concatenate([stat_buf[step][1:2] for step in range(shards)], axis=0)
    factors = jnp.exp(tops - jnp.max(tops, axis=0, keepdims=True))
    factors = factors / jnp.sum(totals * factors, axis=0, keepdims=True)
    short = -shards % 128
    factors = jnp.transpose(
        jnp.concatenate([factors, jnp.zeros((short, factors.shape[1]), f32)], axis=0)
    )
    mixed = mixed * factors[:, 0:1]
    for step, copy in enumerate(mixing, 1):
        copy.wait_recv()
        mixed = mixed + mixed_buf[step].astype(f32) * factors[:, step : step + 1]
    mixed = (mixed * ctx_gain_ref[own]).astype(bf16)
    partial = jnp.concatenate(
        [
            jnp.dot(
                mixed[head * latents : (head + 1) * latents],
                v_ref[:, cut],
                preferred_element_type=f32,
            )
            for head, cut in enumerate(split)
        ],
        axis=1,
    )
    att_stage[...] = partial.astype(bf16)
    moved = ring(5, lambda peer: att_stage, lambda step: att_buf.at[step])
    loads[4].wait()
    arrive(moved)
    attended = summed(partial, att_buf).astype(bf16)
    partial = contract_last(attended, o_ref[...])
    cross_stage[...] = partial.astype(bf16)
    moved = []
    for step in range(1, peers):
        other = lax.rem(spot + step, peers)
        moved.append(
            send(
                cross_stage,
                cross_buf.at[step],
                cross_send.at[step],
                cross_recv.at[step],
                {"tp": other // subs, "sub": lax.rem(other, subs)},
            )
        )
    loads[5].wait()
    arrive(moved)
    hidden = (lat_part + summed(partial, cross_buf)).astype(bf16).astype(f32)
    scaled = (hidden * mid_gain_ref[own]).astype(bf16)
    partials = [
        jnp.dot(scaled, qkv_ref[index], preferred_element_type=f32) for index in range(3)
    ]
    square = jnp.sum(hidden * hidden, axis=1, keepdims=True)
    coarse = square.astype(bf16).astype(f32)
    lane = lax.broadcasted_iota(jnp.int32, (latents, 128), 1)
    square = jnp.where(lane == 0, coarse, jnp.where(lane == 1, square - coarse, 0.0))
    for head, cut in enumerate(split):
        proj_stage[head] = jnp.concatenate(
            [part[:, cut] for part in partials] + [square], axis=1
        ).astype(bf16)
    moved = ring(6, lambda peer: proj_stage.at[peer], lambda step: proj_buf.at[step])
    total = proj_stage[own].astype(f32)
    loads[6].wait()
    arrive(moved)
    total = summed(total, proj_buf)
    square = total[:, 3 * DH : 3 * DH + 1] + total[:, 3 * DH + 1 : 3 * DH + 2]
    projected = (total[:, : 3 * DH] * lax.rsqrt(square / width + EPS)).astype(bf16)
    causal = lax.broadcasted_iota(jnp.int32, (latents, latents), 1) <= lax.broadcasted_iota(
        jnp.int32, (latents, latents), 0
    )
    scores = contract_last(projected[:, :DH], projected[:, DH : 2 * DH]) * (1.0 / math.sqrt(DH))
    scores = jnp.where(causal, scores, NEG)
    weights = jnp.where(causal, jnp.exp(scores - jnp.max(scores, axis=1, keepdims=True)), 0.0)
    numerator = jnp.dot(
        weights.astype(bf16), projected[:, 2 * DH :], preferred_element_type=f32
    )
    self_buf[own] = (numerator / jnp.sum(weights, axis=1, keepdims=True)).astype(bf16)
    arrive(ring(7, lambda peer: self_buf.at[own], lambda step: self_buf.at[own]))
    attended = jnp.concatenate([self_buf[head] for head in range(heads)], axis=1)
    partial = contract_last(attended, last_ref[...])
    partial = partial + hidden * jnp.where(spot == 0, 1.0, 0.0).astype(f32)

    goal = own // ratio
    slot = lax.rem(own, ratio) * peers + spot
    for shard in range(shards):
        end_stage[shard] = partial[shard * rows : (shard + 1) * rows]

    def hand(step):
        other = lax.rem(own + step, shards)
        return pltpu.make_async_remote_copy(
            src_ref=end_stage.at[other],
            dst_ref=end_buf.at[slot],
            send_sem=end_send.at[step],
            recv_sem=end_recv.at[slot],
            device_id={"ctx": other, "tp": goal // subs, "sub": lax.rem(goal, subs)},
            device_id_type=MESH,
        )

    for step in range(1, shards):
        hand(step).start()

    @pl.when(goal != spot)
    def _():
        hand(0).start()

    @pl.when(goal == spot)
    def _():
        end_buf[slot] = end_stage[own]

    for inside in range(ratio):
        for source in range(peers):
            at = inside * peers + source

            @pl.when(jnp.logical_or(spot * ratio + inside != own, spot != source))
            def _():
                pltpu.make_async_remote_copy(
                    src_ref=end_stage.at[0],
                    dst_ref=end_buf.at[at],
                    send_sem=end_send.at[0],
                    recv_sem=end_recv.at[at],
                    device_id={"ctx": lax.rem(own + 1, shards)},
                    device_id_type=MESH,
                ).wait_recv()

    for inside in range(ratio):
        first = end_buf[inside * peers]
        for source in range(1, peers):
            first = first + end_buf[inside * peers + source]
        result_ref[:, inside * depth : (inside + 1) * depth] = first.astype(bf16)
    for copy in started:
        copy.wait_send()
    for step in range(1, shards):
        hand(step).wait_send()

    @pl.when(goal != spot)
    def _():
        hand(0).wait_send()


def fused(
    context,
    context_pos,
    latent_in,
    latent_start,
    ctx_gain,
    lat_gain,
    mid_gain,
    cross_q,
    cross_k,
    cross_v,
    cross_out,
    self_qkv,
    self_out,
):
    rows, width = latent_in.shape
    depth, columns = cross_q.shape
    tokens = context.shape[0]
    shards, tps, subs = lax.axis_size("ctx"), lax.axis_size("tp"), lax.axis_size("sub")
    peers = tps * subs
    latents = rows * shards
    lines = columns // DH * latents
    ends = columns // depth * peers
    f32, bf16 = jnp.float32, jnp.bfloat16
    vmem, dma = pltpu.VMEM, pltpu.SemaphoreType.DMA
    held = pl.BlockSpec(memory_space=pltpu.VMEM)
    away = pl.BlockSpec(memory_space=pl.ANY)
    return pl.pallas_call(
        step_kernel,
        out_shape=jax.ShapeDtypeStruct((rows, columns), bf16),
        in_specs=[pl.BlockSpec(memory_space=pltpu.SMEM)] + [held] * 5 + [away] * 7,
        out_specs=held,
        scratch_shapes=[
            vmem((peers, tokens, columns), bf16),
            vmem((depth, columns), bf16),
            vmem((depth, columns), bf16),
            vmem((depth, columns), bf16),
            vmem((depth, columns), bf16),
            vmem((3, depth, columns), bf16),
            vmem((depth, columns), bf16),
            vmem((shards, 2 * rows, depth), bf16),
            vmem((shards, 2 * rows, depth), bf16),
            vmem((latents, columns), bf16),
            vmem((shards, latents, columns), bf16),
            vmem((shards, lines, depth), bf16),
            vmem((8, lines), f32),
            vmem((shards, 8, lines), f32),
            vmem((shards, lines, depth), bf16),
            vmem((shards, lines, depth), bf16),
            vmem((latents, columns), bf16),
            vmem((shards, latents, columns), bf16),
            vmem((latents, depth), bf16),
            vmem((peers, latents, depth), bf16),
            vmem((shards, latents, 4 * DH), bf16),
            vmem((shards, latents, 4 * DH), bf16),
            vmem((shards, latents, DH), bf16),
            vmem((shards, rows, depth), f32),
            vmem((ends, rows, depth), f32),
            dma((7,)),
            dma((8, shards)),
            dma((8, shards)),
            dma((tps + 1, max(tps, subs), CHUNKS)),
            dma((tps + 1, max(tps, subs), CHUNKS)),
            dma((peers,)),
            dma((peers,)),
            dma((shards,)),
            dma((ends,)),
        ],
        compiler_params=pltpu.CompilerParams(
            collective_id=0, has_side_effects=True, vmem_limit_bytes=56 << 20
        ),
    )(
        latent_start,
        context_pos,
        latent_in,
        ctx_gain.reshape(shards, 1, depth),
        lat_gain.reshape(shards, 1, depth),
        mid_gain.reshape(shards, 1, depth),
        context,
        cross_q,
        cross_k,
        cross_v,
        cross_out,
        jnp.transpose(self_qkv, (1, 0, 2)),
        self_out,
    )


def on_device(*arrays):
    depth, columns = arrays[7].shape
    if depth == columns == lax.axis_size("ctx") * DH:
        return fused(*arrays)
    return collectives(*arrays)


def solution(mesh):
    return jax.shard_map(
        on_device,
        mesh=mesh,
        in_specs=(
            P(("grp", "ctx"), ("tp", "sub")),
            P(("grp", "ctx")),
            P(("grp", "ctx"), None),
            P("grp"),
            P(),
            P(),
            P(),
            P("ctx", ("tp", "sub")),
            P("ctx", ("tp", "sub")),
            P("ctx", ("tp", "sub")),
            P("ctx", ("tp", "sub")),
            P("ctx", None, ("tp", "sub")),
            P("ctx", ("tp", "sub")),
        ),
        out_specs=P(("grp", "ctx"), ("tp", "sub")),
        check_vma=False,
    )
```

```python
import math

import jax
import jax.numpy as jnp
from jax import lax
from jax.experimental import pallas as pl
from jax.experimental.pallas import tpu as pltpu
from jax.sharding import PartitionSpec as P

DH = 128


EPS = 1e-05
NEG = -1e30
HEADS_AXES = ("tp", "sub")
MESH = pl.DeviceIdType.MESH
CHUNKS = 4


def contract_last(left, right):
    return lax.dot_general(
        left, right, (((1,), (1,)), ((), ())), preferred_element_type=jnp.float32
    )


def summed_over(partial, axis):
    everything = lax.all_gather(partial.astype(jnp.bfloat16), axis)
    return jnp.sum(everything.astype(jnp.float32), axis=0)


def collectives(
    context,
    context_pos,
    latent_in,
    latent_start,
    ctx_gain,
    lat_gain,
    mid_gain,
    cross_q,
    cross_k,
    cross_v,
    cross_out,
    self_qkv,
    self_out,
):
    rows, width = latent_in.shape
    depth, columns = cross_q.shape
    shards = lax.axis_size("ctx")
    heads = columns // DH
    latents = rows * shards
    own = lax.axis_index("ctx")
    mine = lambda array: lax.dynamic_slice_in_dim(array, own * depth, depth, array.ndim - 1)
    whole = lax.all_gather(context, HEADS_AXES, axis=1, tiled=True)
    all_latents = lax.all_gather(latent_in, "ctx", axis=0, tiled=True).astype(jnp.float32)
    lat_scale = lax.rsqrt(jnp.mean(all_latents * all_latents, axis=1, keepdims=True) + EPS)
    lat_part = mine(all_latents)
    normed_lat = (lat_part * lat_scale * mine(lat_gain)).astype(jnp.bfloat16)
    queries = summed_over(
        jnp.dot(normed_lat, cross_q, preferred_element_type=jnp.float32), "ctx"
    ).astype(jnp.bfloat16)
    split = [slice(head * DH, head * DH + DH) for head in range(heads)]
    absorbed = jnp.concatenate(
        [contract_last(queries[:, cut], cross_k[:, cut]) for cut in split], axis=0
    )
    absorbed = (absorbed * (mine(ctx_gain) * (1.0 / math.sqrt(DH)))).astype(jnp.bfloat16)
    absorbed = lax.all_gather(absorbed, "ctx", axis=1, tiled=True)

    wide = whole.astype(jnp.float32)
    token_scale = lax.rsqrt(jnp.mean(wide * wide, axis=1) + EPS)
    scores = contract_last(absorbed, whole) * token_scale[None, :]
    query_pos = latent_start[0] + jnp.arange(latents, dtype=jnp.int32)
    allowed = jnp.tile(context_pos[None, :] <= query_pos[:, None], (heads, 1))
    scores = jnp.where(allowed, scores, NEG)
    top = jnp.max(scores, axis=1, keepdims=True)
    weights = jnp.where(allowed, jnp.exp(scores - top), 0.0)
    total = jnp.sum(weights, axis=1, keepdims=True)
    mixed = jnp.dot(
        (weights * token_scale[None, :]).astype(jnp.bfloat16),
        whole,
        preferred_element_type=jnp.float32,
    ).astype(jnp.bfloat16)
    mixed = lax.all_to_all(
        mixed.reshape(heads * latents, shards, depth), "ctx", split_axis=1, concat_axis=0
    ).reshape(shards, heads * latents, depth)
    stats = lax.all_gather(jnp.concatenate([top, total], axis=1), "ctx")
    tops, totals = stats[:, :, :1], stats[:, :, 1:]
    factors = jnp.exp(tops - jnp.max(tops, axis=0))
    mixed = jnp.sum(mixed.astype(jnp.float32) * factors, axis=0) / jnp.sum(totals * factors, axis=0)
    mixed = (mixed * mine(ctx_gain)).astype(jnp.bfloat16)
    attended = jnp.concatenate(
        [
            jnp.dot(
                mixed[head * latents : (head + 1) * latents],
                cross_v[:, cut],
                preferred_element_type=jnp.float32,
            )
            for head, cut in enumerate(split)
        ],
        axis=1,
    )
    attended = summed_over(attended, "ctx").astype(jnp.bfloat16)
    cross_sum = summed_over(contract_last(attended, cross_out), HEADS_AXES)
    hidden = (lat_part + cross_sum).astype(jnp.bfloat16).astype(jnp.float32)
    squares = jnp.sum(lax.all_gather(jnp.sum(hidden * hidden, axis=1), "ctx"), axis=0)
    hidden_scale = lax.rsqrt(squares / width + EPS)
    projected = jnp.dot(
        (hidden * mine(mid_gain)).astype(jnp.bfloat16),
        self_qkv.reshape(depth, 3 * columns),
        preferred_element_type=jnp.float32,
    )
    projected = summed_over(projected, "ctx") * hidden_scale[:, None]
    projected = projected.astype(jnp.bfloat16).reshape(latents, 3, columns)
    index = jnp.arange(latents, dtype=jnp.int32)
    causal = index[None, :] <= index[:, None]
    parts = []
    for cut in split:
        scores = contract_last(projected[:, 0, cut], projected[:, 1, cut]) * (1.0 / math.sqrt(DH))
        scores = jnp.where(causal, scores, NEG)
        weights = jnp.where(causal, jnp.exp(scores - jnp.max(scores, axis=1, keepdims=True)), 0.0)
        numerator = jnp.dot(
            weights.astype(jnp.bfloat16), projected[:, 2, cut], preferred_element_type=jnp.float32
        )
        parts.append(numerator / jnp.sum(weights, axis=1, keepdims=True))
    attended_self = jnp.concatenate(parts, axis=1).astype(jnp.bfloat16)
    self_sum = summed_over(contract_last(attended_self, self_out), HEADS_AXES)
    result = (hidden + self_sum).astype(jnp.bfloat16)
    result = lax.all_to_all(
        result.reshape(shards, rows, depth), "ctx", split_axis=0, concat_axis=1
    ).reshape(rows, width)
    return lax.dynamic_slice_in_dim(result, lax.axis_index(HEADS_AXES) * columns, columns, 1)


def step_kernel(
    start_ref,
    pos_ref,
    latent_ref,
    ctx_gain_ref,
    lat_gain_ref,
    mid_gain_ref,
    context_ref,
    q_hbm,
    k_hbm,
    v_hbm,
    out_hbm,
    qkv_hbm,
    last_hbm,
    result_ref,
    ctx_buf,
    q_ref,
    k_ref,
    v_ref,
    o_ref,
    qkv_ref,
    last_ref,
    lat_stage,
    lat_buf,
    query_stage,
    query_buf,
    absorbed_buf,
    stat_stage,
    stat_buf,
    mixed_stage,
    mixed_buf,
    att_stage,
    att_buf,
    cross_stage,
    cross_buf,
    proj_stage,
    proj_buf,
    self_buf,
    end_stage,
    end_buf,
    load_sem,
    ring_send,
    ring_recv,
    ctx_send,
    ctx_recv,
    cross_send,
    cross_recv,
    end_send,
    end_recv,
):
    shards, tps, subs = lax.axis_size("ctx"), lax.axis_size("tp"), lax.axis_size("sub")
    peers = tps * subs
    own, tp, sub = lax.axis_index("ctx"), lax.axis_index("tp"), lax.axis_index("sub")
    spot = tp * subs + sub
    rows, width = latent_ref.shape
    depth, columns = q_ref.shape
    heads = columns // DH
    latents = rows * shards
    tokens = context_ref.shape[0]
    ratio = columns // depth
    f32, bf16 = jnp.float32, jnp.bfloat16
    split = [slice(head * DH, head * DH + DH) for head in range(heads)]

    loads = [
        pltpu.make_async_copy(source, target, load_sem.at[index])
        for index, (source, target) in enumerate(
            (
                (context_ref, ctx_buf.at[spot]),
                (q_hbm, q_ref),
                (k_hbm, k_ref),
                (v_hbm, v_ref),
                (out_hbm, o_ref),
                (qkv_hbm, qkv_ref),
                (last_hbm, last_ref),
            )
        )
    ]
    for load in loads:
        load.start()

    barrier = pltpu.get_barrier_semaphore()
    everyone = shards * peers
    me = own * peers + spot
    for step in range(1, everyone):
        other = lax.rem(me + step, everyone)
        pl.semaphore_signal(
            barrier,
            inc=1,
            device_id={
                "ctx": other // peers,
                "tp": lax.rem(other, peers) // subs,
                "sub": lax.rem(other, subs),
            },
            device_id_type=MESH,
        )

    wide = latent_ref[...].astype(f32)
    scale = lax.rsqrt(jnp.mean(wide * wide, axis=1, keepdims=True) + EPS)
    for shard in range(shards):
        part = wide[:, shard * depth : (shard + 1) * depth]
        lat_stage[shard] = jnp.concatenate(
            [part, part * scale * lat_gain_ref[shard]], axis=0
        ).astype(bf16)
    pl.semaphore_wait(barrier, everyone - 1)

    started = []

    def send(source, target, send_sem, recv_sem, device):
        copy = pltpu.make_async_remote_copy(
            src_ref=source,
            dst_ref=target,
            send_sem=send_sem,
            recv_sem=recv_sem,
            device_id=device,
            device_id_type=MESH,
        )
        copy.start()
        started.append(copy)
        return copy

    def ring(phase, pick, target):
        return [
            send(
                pick(lax.rem(own + step, shards)),
                target(step),
                ring_send.at[phase, step],
                ring_recv.at[phase, step],
                {"ctx": lax.rem(own + step, shards)},
            )
            for step in range(1, shards)
        ]

    def arrive(copies):
        for copy in copies:
            copy.wait_recv()

    def summed(first, buf):
        for step in range(1, buf.shape[0]):
            first = first + buf[step].astype(f32)
        return first

    moved = ring(0, lambda peer: lat_stage.at[peer], lambda step: lat_buf.at[own])
    chunk = tokens // CHUNKS
    pieces = [pl.ds(piece * chunk, chunk) for piece in range(CHUNKS)]
    across = [
        [
            send(
                context_ref.at[piece],
                ctx_buf.at[spot, piece],
                ctx_send.at[0, step, at],
                ctx_recv.at[0, step, at],
                {"tp": lax.rem(tp + step, tps)},
            )
            for step in range(1, tps)
        ]
        for at, piece in enumerate(pieces)
    ]
    beside = [
        send(
            context_ref,
            ctx_buf.at[spot],
            ctx_send.at[tps, step, 0],
            ctx_recv.at[tps, step, 0],
            {"sub": lax.rem(sub + step, subs)},
        )
        for step in range(1, subs)
    ]

    def forward(at):
        handed = []
        for step, copy in enumerate(across[at], 1):
            copy.wait_recv()
            block = lax.rem(tp + tps - step, tps) * subs + sub
            handed = handed + [
                send(
                    ctx_buf.at[block, pieces[at]],
                    ctx_buf.at[block, pieces[at]],
                    ctx_send.at[step, hop, at],
                    ctx_recv.at[step, hop, at],
                    {"sub": lax.rem(sub + hop, subs)},
                )
                for hop in range(1, subs)
            ]
        return handed

    lat_buf[own] = lat_stage[own]
    loads[1].wait()
    arrive(moved)
    blocks = [lat_buf[shard].astype(f32) for shard in range(shards)]
    lat_part = jnp.concatenate([block[:rows] for block in blocks], axis=0)
    normed = jnp.concatenate([block[rows:] for block in blocks], axis=0).astype(bf16)
    partial = jnp.dot(normed, q_ref[...], preferred_element_type=f32)
    query_stage[...] = partial.astype(bf16)
    moved = ring(1, lambda peer: query_stage, lambda step: query_buf.at[step])
    beside = beside + forward(0)
    loads[2].wait()
    arrive(moved)
    beside = beside + forward(1)
    queries = summed(partial, query_buf).astype(bf16)
    absorbed = jnp.concatenate(
        [contract_last(queries[:, cut], k_ref[:, cut]) for cut in split], axis=0
    )
    absorbed_buf[own] = (absorbed * (ctx_gain_ref[own] * (1.0 / math.sqrt(DH)))).astype(bf16)
    moved = ring(2, lambda peer: absorbed_buf.at[own], lambda step: absorbed_buf.at[own])

    for at in range(2, CHUNKS):
        beside = beside + forward(at)
    loads[0].wait()
    arrive(beside)
    squares = jnp.zeros((8, tokens), f32)
    for block in range(peers):
        wide = ctx_buf[block].astype(f32)
        squares = squares + lax.dot_general(
            jnp.ones((8, columns), f32),
            wide * wide,
            (((1,), (1,)), ((), ())),
            precision=lax.Precision.HIGHEST,
            preferred_element_type=f32,
        )
    token_scale = lax.rsqrt(squares[:1] / width + EPS)
    query_pos = start_ref[...].reshape(1, 1) + lax.broadcasted_iota(jnp.int32, (latents, tokens), 0)
    query_pos = jnp.concatenate([query_pos] * heads, axis=0)
    allowed = jnp.broadcast_to(pos_ref[...].reshape(1, tokens), query_pos.shape) <= query_pos
    scores = contract_last(absorbed_buf[own], ctx_buf[own])
    for step, copy in enumerate(moved, 1):
        copy.wait_recv()
        source = lax.rem(own + shards - step, shards)
        scores = scores + contract_last(absorbed_buf[source], ctx_buf[source])
    scores = jnp.where(allowed, scores * token_scale, NEG)
    top = jnp.max(scores, axis=1, keepdims=True)
    weights = jnp.where(allowed, jnp.exp(scores - top), 0.0)
    total = jnp.sum(weights, axis=1, keepdims=True)
    lane = lax.broadcasted_iota(jnp.int32, (heads * latents, 128), 1)
    stat_stage[...] = jnp.transpose(jnp.where(lane == 0, top, total))[:8]
    moved = ring(3, lambda peer: stat_stage, lambda step: stat_buf.at[step])
    scaled = (weights * token_scale).astype(bf16)
    mixing = []
    for step in range(1, shards):
        other = lax.rem(own + step, shards)
        mixed_stage[step] = jnp.dot(
            scaled, ctx_buf[other], preferred_element_type=f32
        ).astype(bf16)
        mixing.append(
            send(
                mixed_stage.at[step],
                mixed_buf.at[step],
                ring_send.at[4, step],
                ring_recv.at[4, step],
                {"ctx": other},
            )
        )
    mixed = jnp.dot(scaled, ctx_buf[own], preferred_element_type=f32)
    stat_buf[0] = stat_stage[...]
    loads[3].wait()
    arrive(moved)
    tops = jnp.concatenate([stat_buf[step][0:1] for step in range(shards)], axis=0)
    totals = jnp.concatenate([stat_buf[step][1:2] for step in range(shards)], axis=0)
    factors = jnp.exp(tops - jnp.max(tops, axis=0, keepdims=True))
    factors = factors / jnp.sum(totals * factors, axis=0, keepdims=True)
    short = -shards % 128
    factors = jnp.transpose(
        jnp.concatenate([factors, jnp.zeros((short, factors.shape[1]), f32)], axis=0)
    )
    mixed = mixed * factors[:, 0:1]
    for step, copy in enumerate(mixing, 1):
        copy.wait_recv()
        mixed = mixed + mixed_buf[step].astype(f32) * factors[:, step : step + 1]
    mixed = (mixed * ctx_gain_ref[own]).astype(bf16)
    partial = jnp.concatenate(
        [
            jnp.dot(
                mixed[head * latents : (head + 1) * latents],
                v_ref[:, cut],
                preferred_element_type=f32,
            )
            for head, cut in enumerate(split)
        ],
        axis=1,
    )
    att_stage[...] = partial.astype(bf16)
    moved = ring(5, lambda peer: att_stage, lambda step: att_buf.at[step])
    loads[4].wait()
    arrive(moved)
    attended = summed(partial, att_buf).astype(bf16)
    partial = contract_last(attended, o_ref[...])
    cross_stage[...] = partial.astype(bf16)
    moved = []
    for step in range(1, peers):
        other = lax.rem(spot + step, peers)
        moved.append(
            send(
                cross_stage,
                cross_buf.at[step],
                cross_send.at[step],
                cross_recv.at[step],
                {"tp": other // subs, "sub": lax.rem(other, subs)},
            )
        )
    loads[5].wait()
    arrive(moved)
    hidden = (lat_part + summed(partial, cross_buf)).astype(bf16).astype(f32)
    scaled = (hidden * mid_gain_ref[own]).astype(bf16)
    partials = [
        jnp.dot(scaled, qkv_ref[index], preferred_element_type=f32) for index in range(3)
    ]
    square = jnp.sum(hidden * hidden, axis=1, keepdims=True)
    coarse = square.astype(bf16).astype(f32)
    lane = lax.broadcasted_iota(jnp.int32, (latents, 128), 1)
    square = jnp.where(lane == 0, coarse, jnp.where(lane == 1, square - coarse, 0.0))
    for head, cut in enumerate(split):
        proj_stage[head] = jnp.concatenate(
            [part[:, cut] for part in partials] + [square], axis=1
        ).astype(bf16)
    moved = ring(6, lambda peer: proj_stage.at[peer], lambda step: proj_buf.at[step])
    total = proj_stage[own].astype(f32)
    loads[6].wait()
    arrive(moved)
    total = summed(total, proj_buf)
    square = total[:, 3 * DH : 3 * DH + 1] + total[:, 3 * DH + 1 : 3 * DH + 2]
    projected = (total[:, : 3 * DH] * lax.rsqrt(square / width + EPS)).astype(bf16)
    causal = lax.broadcasted_iota(jnp.int32, (latents, latents), 1) <= lax.broadcasted_iota(
        jnp.int32, (latents, latents), 0
    )
    scores = contract_last(projected[:, :DH], projected[:, DH : 2 * DH]) * (1.0 / math.sqrt(DH))
    scores = jnp.where(causal, scores, NEG)
    weights = jnp.where(causal, jnp.exp(scores - jnp.max(scores, axis=1, keepdims=True)), 0.0)
    numerator = jnp.dot(
        weights.astype(bf16), projected[:, 2 * DH :], preferred_element_type=f32
    )
    self_buf[own] = (numerator / jnp.sum(weights, axis=1, keepdims=True)).astype(bf16)
    arrive(ring(7, lambda peer: self_buf.at[own], lambda step: self_buf.at[own]))
    attended = jnp.concatenate([self_buf[head] for head in range(heads)], axis=1)
    partial = contract_last(attended, last_ref[...])
    partial = partial + hidden * jnp.where(spot == 0, 1.0, 0.0).astype(f32)

    goal = own // ratio
    slot = lax.rem(own, ratio) * peers + spot
    for shard in range(shards):
        end_stage[shard] = partial[shard * rows : (shard + 1) * rows].astype(bf16)

    def hand(step):
        other = lax.rem(own + step, shards)
        return pltpu.make_async_remote_copy(
            src_ref=end_stage.at[other],
            dst_ref=end_buf.at[slot],
            send_sem=end_send.at[step],
            recv_sem=end_recv.at[slot],
            device_id={"ctx": other, "tp": goal // subs, "sub": lax.rem(goal, subs)},
            device_id_type=MESH,
        )

    for step in range(1, shards):
        hand(step).start()

    @pl.when(goal != spot)
    def _():
        hand(0).start()

    @pl.when(goal == spot)
    def _():
        end_buf[slot] = end_stage[own]

    for inside in range(ratio):
        for source in range(peers):
            at = inside * peers + source

            @pl.when(jnp.logical_or(spot * ratio + inside != own, spot != source))
            def _():
                pltpu.make_async_remote_copy(
                    src_ref=end_stage.at[0],
                    dst_ref=end_buf.at[at],
                    send_sem=end_send.at[0],
                    recv_sem=end_recv.at[at],
                    device_id={"ctx": lax.rem(own + 1, shards)},
                    device_id_type=MESH,
                ).wait_recv()

    for inside in range(ratio):
        first = end_buf[inside * peers].astype(f32)
        for source in range(1, peers):
            first = first + end_buf[inside * peers + source].astype(f32)
        result_ref[:, inside * depth : (inside + 1) * depth] = first.astype(bf16)
    for copy in started:
        copy.wait_send()
    for step in range(1, shards):
        hand(step).wait_send()

    @pl.when(goal != spot)
    def _():
        hand(0).wait_send()


def fused(
    context,
    context_pos,
    latent_in,
    latent_start,
    ctx_gain,
    lat_gain,
    mid_gain,
    cross_q,
    cross_k,
    cross_v,
    cross_out,
    self_qkv,
    self_out,
):
    rows, width = latent_in.shape
    depth, columns = cross_q.shape
    tokens = context.shape[0]
    shards, tps, subs = lax.axis_size("ctx"), lax.axis_size("tp"), lax.axis_size("sub")
    peers = tps * subs
    latents = rows * shards
    lines = columns // DH * latents
    ends = columns // depth * peers
    f32, bf16 = jnp.float32, jnp.bfloat16
    vmem, dma = pltpu.VMEM, pltpu.SemaphoreType.DMA
    held = pl.BlockSpec(memory_space=pltpu.VMEM)
    away = pl.BlockSpec(memory_space=pl.ANY)
    return pl.pallas_call(
        step_kernel,
        out_shape=jax.ShapeDtypeStruct((rows, columns), bf16),
        in_specs=[held] * 6 + [away] * 7,
        out_specs=held,
        scratch_shapes=[
            vmem((peers, tokens, columns), bf16),
            vmem((depth, columns), bf16),
            vmem((depth, columns), bf16),
            vmem((depth, columns), bf16),
            vmem((depth, columns), bf16),
            vmem((3, depth, columns), bf16),
            vmem((depth, columns), bf16),
            vmem((shards, 2 * rows, depth), bf16),
            vmem((shards, 2 * rows, depth), bf16),
            vmem((latents, columns), bf16),
            vmem((shards, latents, columns), bf16),
            vmem((shards, lines, depth), bf16),
            vmem((8, lines), f32),
            vmem((shards, 8, lines), f32),
            vmem((shards, lines, depth), bf16),
            vmem((shards, lines, depth), bf16),
            vmem((latents, columns), bf16),
            vmem((shards, latents, columns), bf16),
            vmem((latents, depth), bf16),
            vmem((peers, latents, depth), bf16),
            vmem((shards, latents, 4 * DH), bf16),
            vmem((shards, latents, 4 * DH), bf16),
            vmem((shards, latents, DH), bf16),
            vmem((shards, rows, depth), bf16),
            vmem((ends, rows, depth), bf16),
            dma((7,)),
            dma((8, shards)),
            dma((8, shards)),
            dma((tps + 1, max(tps, subs), CHUNKS)),
            dma((tps + 1, max(tps, subs), CHUNKS)),
            dma((peers,)),
            dma((peers,)),
            dma((shards,)),
            dma((ends,)),
        ],
        compiler_params=pltpu.CompilerParams(
            collective_id=0, has_side_effects=True, vmem_limit_bytes=56 << 20
        ),
    )(
        latent_start,
        context_pos,
        latent_in,
        ctx_gain.reshape(shards, 1, depth),
        lat_gain.reshape(shards, 1, depth),
        mid_gain.reshape(shards, 1, depth),
        context,
        cross_q,
        cross_k,
        cross_v,
        cross_out,
        jnp.transpose(self_qkv, (1, 0, 2)),
        self_out,
    )


def on_device(*arrays):
    depth, columns = arrays[7].shape
    if depth == columns == lax.axis_size("ctx") * DH:
        return fused(*arrays)
    return collectives(*arrays)


def solution(mesh):
    return jax.shard_map(
        on_device,
        mesh=mesh,
        in_specs=(
            P(("grp", "ctx"), ("tp", "sub")),
            P(("grp", "ctx")),
            P(("grp", "ctx"), None),
            P("grp"),
            P(),
            P(),
            P(),
            P("ctx", ("tp", "sub")),
            P("ctx", ("tp", "sub")),
            P("ctx", ("tp", "sub")),
            P("ctx", ("tp", "sub")),
            P("ctx", None, ("tp", "sub")),
            P("ctx", ("tp", "sub")),
        ),
        out_specs=P(("grp", "ctx"), ("tp", "sub")),
        check_vma=False,
    )
```
